32 devices in a mesh: gx: 8 (over y, x, core), gy: 4 (over z).
Axes of the slice: x: 2, y: 2, z: 4, core: 2. Of those that a mesh axis runs over, the one named last changes fastest.
Arguments:
- tokens: bfloat16 [4096, 2048], P(('gx', 'gy')), may hold values from -6 to 6
- expert_ids: int32 [4096, 8], P(('gx', 'gy')), may hold values from 0 to 31, all different within a row; in each aligned block of 128 rows (0 to 127, 128 to 255, ...) at most 96 rows name the same one
- w_gate: bfloat16 [32, 2048, 768], P(('gx', 'gy')), may hold values from -0.125 to 0.125
- w_up: bfloat16 [32, 2048, 768], P(('gx', 'gy')), may hold values from -0.125 to 0.125
- down_error: float32 [32, 768, 2048], P(('gx', 'gy')), may hold values from -18 to 18
Outputs:
- gram_error: float32 [32, 768, 2048], P(('gx', 'gy'))
The draws below stay inside these ranges and needn't reach their ends.
Inputs may be any that keep to these rules, and one draw needn't show every extreme that they name: `expert_ids`: among the rows of one device no expert is named more than 96 times, a bound that some block reaches; every expert is named by some row; the 8 ids of a row are distinct.
All inputs are finite; a program needn't handle non-finite values.
Results may differ from the reference program's by a relative error of at most 0.0036.
Values may be sent and summed in bfloat16 or wider, within the bound.
A program may use at most 128 MiB of HBM per device.

```python
import math
import jax
import jax.numpy as jnp
import numpy as np
from jax import lax

D = 2048
FF = 768
TOP = 8
TOK_DEV = 128
EXPERTS = 32
TOKENS = 4096
CAP = 96


def shard_levels(stream_key, dims, pieces, low, top_value):
    def one(position, blocks):
        heights = jax.random.uniform(jax.random.fold_in(jax.random.fold_in(stream_key, 6), position), (blocks,), jnp.float32, low / len(pieces), top_value / len(pieces))
        return jnp.repeat(jnp.exp(heights), dims[position] // blocks).reshape((-1,) + (1,) * (len(dims) - position - 1))

    factor_of = one(*pieces[0])
    for cut in pieces[1:]:
        factor_of = factor_of * one(*cut)
    return factor_of


def shared_out(own_key, own, number, rows, count, top, limit, skew):
    sequence = jax.random.permutation(own_key, count)
    packed, ordinary = portions_of(count, rows * top, limit, skew, True), portions_of(count, rows * top, limit, skew, False)
    places = jnp.arange(count)

    def named(sizes, offset_by):
        used = int((sizes > 0).sum())
        fixed = max(1, used // 4)
        shifted = fixed + (places - fixed + offset_by * (used - fixed)) % max(1, count - fixed)
        return jnp.zeros((count,), jnp.int32).at[sequence[jnp.where(places < fixed, places, shifted)]].set(jnp.asarray(sizes, jnp.int32))

    sizes = jnp.where(number % 4 == 0, named(packed, number // 4), named(ordinary, number - number // 4 - 1))
    mixed = jax.random.permutation(jax.random.fold_in(own, 3), count)
    source_of, sink = mixed[0:count // 2 * 2:2], mixed[1:count // 2 * 2:2]
    room = jnp.minimum(sizes[source_of] - 1, limit - sizes[sink]) // 2
    room = jnp.where((source_of == sequence[0]) | (sink == sequence[0]) | (sizes[sink] == 0), 0, jnp.maximum(room, 0))
    shifted = jax.random.randint(jax.random.fold_in(own, 4), (count // 2,), 0, 1 << 20) % (room + 1)
    sizes = sizes.at[source_of].add(-shifted).at[sink].add(shifted)
    items = jnp.searchsorted(jnp.cumsum(sizes), jnp.arange(rows * top), side="right").astype(jnp.int32)
    table = items.reshape(top, rows).T
    table = table[jax.random.permutation(jax.random.fold_in(own, 1), rows)]
    offset_by = jax.random.randint(jax.random.fold_in(own, 2), (rows, 1), 0, top)
    return jnp.take_along_axis(table, (jnp.arange(top)[None, :] + offset_by) % top, axis=1)


def portions_of(number_of, total, limit, lean, full):
    weights = [(1 << 20) // math.isqrt(grade ** lean) + 1 for grade in range(1, number_of + 1)]
    largest = limit if full else min(limit, max(-(-total // number_of), total * weights[0] // sum(weights)))
    least = 1 if total - largest >= number_of - 1 else 0
    holding, rest = [largest] + [least] * (number_of - 1), total - largest - least * (number_of - 1)
    while rest > 0:
        movable = [i for i in range(1, number_of) if holding[i] < largest] or [i for i in range(1, number_of) if holding[i] < limit]
        mass, remaining = sum([weights[i] for i in movable]), rest
        for i in movable:
            extra = min(limit - holding[i], max(1, remaining * weights[i] // mass), rest)
            holding[i] = holding[i] + extra
            rest = rest - extra
    return np.array(holding)


def normal_values(stream_key, shape, scale, bound, shards=(), kind=jnp.bfloat16):
    factor_of = shard_levels(stream_key, shape, shards, -0.22, 0.18) if shards else 1.0
    drawn = jax.random.normal(stream_key, shape, jnp.float32) * scale * factor_of
    return jnp.minimum(jnp.maximum(drawn, -bound), bound).astype(kind)


def setup_inputs(seed: int = 0) -> dict:
    splits = jax.random.split(jax.random.key(seed), 6)
    tokens = normal_values(splits[0], (TOKENS, D), 1.0, 6.0, ((0, 32),))
    expert_ids_keys = jax.random.split(jax.random.fold_in(splits[1], 1), TOKENS // TOK_DEV)
    expert_ids_turns = jax.random.permutation(jax.random.fold_in(splits[1], 3), TOKENS // TOK_DEV)
    expert_ids = jax.vmap(lambda own, number: shared_out(jax.random.fold_in(splits[1], 2), own, number, TOK_DEV, EXPERTS, TOP, CAP, 2))(expert_ids_keys, expert_ids_turns).reshape((TOKENS, TOP))
    w_gate = normal_values(splits[2], (EXPERTS, D, FF), D ** -0.5, 0.125, ((0, 32),))
    w_up = normal_values(splits[3], (EXPERTS, D, FF), D ** -0.5, 0.125, ((0, 32),))
    down_error = normal_values(splits[4], (EXPERTS, FF, D), 3.0, 18.0, ((0, 32),), jnp.float32)
    return dict(tokens=tokens, expert_ids=expert_ids, w_gate=w_gate, w_up=w_up, down_error=down_error)


def reference(tokens, expert_ids, w_gate, w_up, down_error):
    flat_ids = expert_ids.reshape(-1).astype(jnp.int32)
    total = flat_ids.shape[0]
    block_rows = 256
    ordering = jnp.argsort(flat_ids, stable=True).astype(jnp.int32)
    padded_order = jnp.concatenate([ordering, jnp.zeros((block_rows,), jnp.int32)])
    counts = jnp.sum((flat_ids[:, None] == jnp.arange(EXPERTS, dtype=jnp.int32)[None, :]).astype(jnp.int32), axis=0)
    starts = (jnp.cumsum(counts) - counts).astype(jnp.int32)

    def one_expert(expert):
        start = starts[expert]
        count = counts[expert]
        gate_matrix = w_gate[expert]
        up_matrix = w_up[expert]

        def add_block(number, accum):
            offset = (number * block_rows).astype(jnp.int32)
            window = lax.dynamic_slice(padded_order, (start + offset,), (block_rows,))
            live = (offset + jnp.arange(block_rows, dtype=jnp.int32)) < count
            picked = tokens[window // TOP]
            gate = jnp.dot(picked, gate_matrix, preferred_element_type=jnp.float32)
            upward = jnp.dot(picked, up_matrix, preferred_element_type=jnp.float32)
            hidden = jnp.where(live[:, None], jax.nn.silu(gate) * upward, jnp.zeros_like(gate)).astype(jnp.bfloat16)
            return accum + jnp.dot(hidden.T, hidden, preferred_element_type=jnp.float32)

        blocks = ((count + block_rows - 1) // block_rows).astype(jnp.int32)
        gram = lax.fori_loop(jnp.int32(0), blocks, add_block, jnp.zeros((FF, FF), jnp.float32))
        mean_gram = gram / count.astype(jnp.float32)
        return jnp.dot(mean_gram, down_error[expert], preferred_element_type=jnp.float32, precision=lax.Precision.HIGHEST)

    return lax.map(one_expert, jnp.arange(EXPERTS, dtype=jnp.int32))
```

```python
import jax
import jax.numpy as jnp
from jax import lax
from jax.experimental import pallas as pl
from jax.experimental.pallas import tpu as pltpu
from jax.sharding import PartitionSpec as P

MESH = pl.DeviceIdType.MESH
LANES = 128


def fused_kernel(
    x_ref, wg_hbm, wu_hbm, out_ref,
    tok, wg, wu, hid, acc, cnt,
    recv, precv, s_x, s_y, s_dx, s_dy, s_p, s_up, s_dn, l_sem,
):
    gx = lax.axis_index("gx")
    z = lax.axis_index("gy")
    rows = x_ref.shape[0]
    half = rows // 2
    width = wg.shape[0]
    core = gx % 2
    px = (gx // 2) % 2
    py = gx // 4
    expert = gx * 4 + z

    def plane_of(a, b):
        return b * 2 + a

    here = plane_of(px, py)
    planes = (here, plane_of(1 - px, py), plane_of(px, 1 - py), plane_of(1 - px, 1 - py))

    def dev(a, b, c):
        return b * 4 + a * 2 + c

    x_dev = (dev(1 - px, py, core), z)
    y_dev = (dev(px, 1 - py, core), z)
    p_dev = (dev(px, py, 1 - core), z)
    up_dev = (gx, z + 1)
    dn_dev = (gx, z - 1)

    mirror = z // 2
    inner = z + (3 - 2 * z) * mirror

    def level(k):
        base = k + inner * (1 - 2 * k) * (1 - k // 2)
        return base + (3 - 2 * base) * mirror

    def block(plane, lev, c):
        return tok.at[plane, lev, pl.ds(c * rows, rows), :]

    def piece(plane, lev, h):
        return tok.at[plane, lev, pl.ds(core * rows + h * half, half), :]

    def copy(src, dst, ssem, rsem, to):
        return pltpu.make_async_remote_copy(
            src_ref=src, dst_ref=dst, send_sem=ssem, recv_sem=rsem,
            device_id=to, device_id_type=MESH,
        )

    def col_copy(k, ssem, to, src=None):
        lev = level(k)
        spot = block(here, lev, core)
        return copy(spot if src is None else src, spot, ssem.at[k], recv.at[here, lev, 0], to)

    def diag_x(k):
        lev = level(k)
        spot = piece(planes[2], lev, 0)
        return copy(spot, spot, s_dx.at[k], recv.at[planes[2], lev, 0], x_dev)

    def diag_y(k):
        lev = level(k)
        spot = piece(planes[1], lev, 1)
        return copy(spot, spot, s_dy.at[k], recv.at[planes[1], lev, 1], y_dev)

    def partner_copy(j, k, src=None):
        lev = level(k)
        spot = block(planes[j], lev, core)
        return copy(spot if src is None else src, spot, s_p.at[j, k], precv.at[planes[j], lev], p_dev)

    def wait_block(j, k):
        lev = level(k)
        spot = block(planes[j], lev, core)
        copy(spot, spot, s_p.at[j, k], recv.at[planes[j], lev, 0], p_dev).wait_recv()

    def wait_piece(j, k, h):
        lev = level(k)
        spot = piece(planes[j], lev, h)
        copy(spot, spot, s_p.at[j, k], recv.at[planes[j], lev, h], p_dev).wait_recv()

    def wait_partner(j, k):
        lev = level(k)
        spot = block(planes[j], lev, 1 - core)
        copy(spot, spot, s_p.at[j, k], precv.at[planes[j], lev], p_dev).wait_recv()

    def unit(j, k):
        wait_partner(j, k)
        lev = level(k)
        view = tok.at[planes[j], lev]
        named = view[:, pl.ds(width, LANES)].astype(jnp.float32)
        hit = jnp.max((named == expert.astype(jnp.float32)).astype(jnp.float32), axis=1, keepdims=True)
        cnt[...] += jnp.broadcast_to(jnp.sum(hit, axis=0, keepdims=True), cnt.shape)
        step = hid.shape[1] // 3

        def columns(n, carry):
            cols = pl.ds(pl.multiple_of(n * step, step), step)
            rows_in = view[:, pl.ds(0, width)]
            gate = jnp.dot(rows_in, wg[:, cols], preferred_element_type=jnp.float32)
            upward = jnp.dot(rows_in, wu[:, cols], preferred_element_type=jnp.float32)
            value = gate / (1.0 + jnp.exp(-gate)) * upward
            hid[:, cols] = jnp.where(hit > 0.5, value, 0.0).astype(jnp.bfloat16)
            return carry

        lax.fori_loop(0, 3, columns, 0)

        def bands(n, carry):
            cols = pl.ds(pl.multiple_of(n * step, step), step)
            acc[cols, :] += lax.dot_general(
                hid[:, cols], hid[...], (((0,), (0,)), ((), ())),
                preferred_element_type=jnp.float32,
            )
            return carry

        lax.fori_loop(0, 3, bands, 0)

    barrier = pltpu.get_barrier_semaphore()
    for to in (x_dev, y_dev, p_dev):
        pl.semaphore_signal(barrier, inc=1, device_id=to, device_id_type=MESH)

    @pl.when(z < 3)
    def _():
        pl.semaphore_signal(barrier, inc=1, device_id=up_dev, device_id_type=MESH)

    @pl.when(z > 0)
    def _():
        pl.semaphore_signal(barrier, inc=1, device_id=dn_dev, device_id_type=MESH)

    local = pltpu.make_async_copy(x_ref, block(here, z, core), l_sem.at[0])
    load_g = pltpu.make_async_copy(wg_hbm, wg, l_sem.at[1])
    load_u = pltpu.make_async_copy(wu_hbm, wu, l_sem.at[2])
    local.start()
    load_g.start()
    load_u.start()
    pl.semaphore_wait(barrier, 4 + inner)

    @pl.when(z < 3)
    def _():
        col_copy(0, s_up, up_dev, x_ref).start()

    @pl.when(z > 0)
    def _():
        col_copy(0, s_dn, dn_dev, x_ref).start()

    col_copy(0, s_x, x_dev, x_ref).start()
    col_copy(0, s_y, y_dev, x_ref).start()
    partner_copy(0, 0, x_ref).start()
    acc[...] = jnp.zeros_like(acc)
    cnt[...] = jnp.zeros_like(cnt)
    local.wait()
    load_g.wait()
    load_u.wait()

    def goes_up(k):
        return jnp.logical_and(level(k) < z, z < 3)

    def goes_down(k):
        return jnp.logical_and(level(k) > z, z > 0)

    def column(k):
        wait_block(0, k)

        @pl.when(goes_up(k))
        def _():
            col_copy(k, s_up, up_dev).start()

        @pl.when(goes_down(k))
        def _():
            col_copy(k, s_dn, dn_dev).start()

        col_copy(k, s_x, x_dev).start()
        col_copy(k, s_y, y_dev).start()
        partner_copy(0, k).start()

    def turn(k, carry):
        unit(0, k)
        wait_block(2, k)
        diag_x(k).start()
        wait_block(1, k)
        diag_y(k).start()
        partner_copy(1, k).start()
        partner_copy(2, k).start()

        @pl.when(k < 3)
        def _():
            column(k + 1)

        unit(1, k)
        unit(2, k)
        wait_piece(3, k, 0)
        wait_piece(3, k, 1)
        partner_copy(3, k).start()
        unit(3, k)
        return carry

    lax.fori_loop(0, 4, turn, 0)
    out_ref[...] = acc[...] / cnt[0:1, 0:1]

    @pl.when(z < 3)
    def _():
        col_copy(0, s_up, up_dev).wait_send()

    @pl.when(z > 0)
    def _():
        col_copy(0, s_dn, dn_dev).wait_send()

    def drain(k, carry):
        @pl.when(goes_up(k))
        def _():
            col_copy(k, s_up, up_dev).wait_send()

        @pl.when(goes_down(k))
        def _():
            col_copy(k, s_dn, dn_dev).wait_send()

        col_copy(k, s_x, x_dev).wait_send()
        col_copy(k, s_y, y_dev).wait_send()
        diag_x(k).wait_send()
        diag_y(k).wait_send()
        for j in range(4):
            partner_copy(j, k).wait_send()
        return carry

    lax.fori_loop(0, 4, drain, 0)


def fused_local(tokens, expert_ids, w_gate, w_up, down_error):
    rows, width = tokens.shape
    hidden = w_gate.shape[2]
    named = jnp.pad(
        expert_ids.astype(jnp.bfloat16),
        ((0, 0), (0, LANES - expert_ids.shape[1])),
        constant_values=-1.0,
    )
    packed = jnp.concatenate([tokens, named], axis=1)
    vmem = pl.BlockSpec(memory_space=pltpu.VMEM)
    hbm = pl.BlockSpec(memory_space=pltpu.HBM)
    dma = pltpu.SemaphoreType.DMA
    mean_gram = pl.pallas_call(
        fused_kernel,
        out_shape=jax.ShapeDtypeStruct((hidden, hidden), jnp.float32),
        in_specs=[vmem, hbm, hbm],
        out_specs=vmem,
        scratch_shapes=[
            pltpu.VMEM((4, 4, 2 * rows, width + LANES), jnp.bfloat16),
            pltpu.VMEM((width, hidden), jnp.bfloat16),
            pltpu.VMEM((width, hidden), jnp.bfloat16),
            pltpu.VMEM((2 * rows, hidden), jnp.bfloat16),
            pltpu.VMEM((hidden, hidden), jnp.float32),
            pltpu.VMEM((8, LANES), jnp.float32),
            dma((4, 4, 2)), dma((4, 4)),
            dma((4,)), dma((4,)), dma((4,)), dma((4,)), dma((4, 4)), dma((4,)), dma((4,)),
            dma((3,)),
        ],
        compiler_params=pltpu.CompilerParams(
            collective_id=0, has_side_effects=True, vmem_limit_bytes=56 * 1024 * 1024
        ),
    )(packed, w_gate[0], w_up[0])
    return jnp.dot(mean_gram, down_error[0], preferred_element_type=jnp.float32)[None]


def hidden_rows(received, w_gate, w_up):
    sources, slots, width = received.shape
    flat_rows = received.reshape(sources * slots, width)
    gate = jnp.dot(flat_rows, w_gate[0], preferred_element_type=jnp.float32)
    upward = jnp.dot(flat_rows, w_up[0], preferred_element_type=jnp.float32)
    hidden = (jax.nn.silu(gate) * upward).astype(jnp.bfloat16)
    return hidden.reshape(sources, slots, hidden.shape[1])


def cross_gram(first, second):
    return lax.dot_general(
        first, second, (((0,), (0,)), ((), ())), preferred_element_type=jnp.float32
    )


def gram_of(hidden):
    middle = hidden.shape[1] // 2
    left_part = hidden[:, :middle]
    right_part = hidden[:, middle:]
    upper_left = cross_gram(left_part, left_part)
    upper_right = cross_gram(left_part, right_part)
    lower_right = cross_gram(right_part, right_part)
    top_band = jnp.concatenate([upper_left, upper_right], axis=1)
    bottom_band = jnp.concatenate([upper_right.T, lower_right], axis=1)
    return jnp.concatenate([top_band, bottom_band], axis=0)


def local(tokens, expert_ids, w_gate, w_up, down_error):
    across = lax.axis_size("gx")
    within = lax.axis_size("gy")
    experts = across * within
    tok_count, top_count = expert_ids.shape
    width = tokens.shape[1]
    assigned = tok_count * top_count
    capacity = 3 * assigned // experts
    flat_ids = expert_ids.reshape(assigned)
    onehot = (flat_ids[:, None] == jnp.arange(experts, dtype=jnp.int32)[None, :]).astype(
        jnp.bfloat16
    )
    positions = jnp.arange(assigned, dtype=jnp.int32)
    lower = (positions[:, None] >= positions[None, :]).astype(jnp.bfloat16)
    running = jnp.dot(lower, onehot, preferred_element_type=jnp.float32)
    slot_of = (jnp.sum(running * onehot, axis=1) - 1.0).astype(jnp.int32)
    target = flat_ids * capacity + slot_of
    picked = tokens[positions // top_count]
    outgoing = jnp.zeros((experts * capacity, width), jnp.bfloat16).at[target].set(picked)
    tallies = jnp.sum(onehot.astype(jnp.float32), axis=0)
    loads = lax.psum_scatter(tallies, ("gx", "gy"), scatter_dimension=0, tiled=True)
    hidden = hidden_rows(
        lax.all_to_all(
            outgoing.reshape(experts, capacity, width),
            ("gx", "gy"),
            split_axis=0,
            concat_axis=0,
            tiled=True,
        ),
        w_gate,
        w_up,
    )
    hidden = hidden.reshape(experts * capacity, hidden.shape[2])
    gram = gram_of(hidden)
    mean_gram = gram / loads[0]
    product = jnp.dot(
        mean_gram,
        down_error[0],
        preferred_element_type=jnp.float32,
        precision=lax.Precision.HIGHEST,
    )
    return product[None]


def solution(mesh):
    small = mesh.shape["gx"] == 8 and mesh.shape["gy"] == 4
    return jax.shard_map(
        fused_local if small else local,
        mesh=mesh,
        in_specs=(
            P(("gx", "gy"), None),
            P(("gx", "gy"), None),
            P(("gx", "gy"), None, None),
            P(("gx", "gy"), None, None),
            P(("gx", "gy"), None, None),
        ),
        out_specs=P(("gx", "gy"), None, None),
        check_vma=False,
    )
```

```python
import jax
import jax.numpy as jnp
from jax import lax
from jax.experimental import pallas as pl
from jax.experimental.pallas import tpu as pltpu
from jax.sharding import PartitionSpec as P

MESH = pl.DeviceIdType.MESH
LANES = 128


def fused_kernel(
    x_ref, wg_hbm, wu_hbm, out_ref,
    tok, wg, wu, hid, acc, cnt,
    recv, precv, s_x, s_y, s_dx, s_dy, s_dz, s_p, s_up, s_dn, l_sem,
):
    gx = lax.axis_index("gx")
    z = lax.axis_index("gy")
    rows = x_ref.shape[0]
    half = rows // 2
    width = wg.shape[0]
    core = gx % 2
    px = (gx // 2) % 2
    py = gx // 4
    expert = gx * 4 + z

    def plane_of(a, b):
        return b * 2 + a

    here = plane_of(px, py)
    planes = (here, plane_of(1 - px, py), plane_of(px, 1 - py), plane_of(1 - px, 1 - py))

    def dev(a, b, c):
        return b * 4 + a * 2 + c

    x_dev = (dev(1 - px, py, core), z)
    y_dev = (dev(px, 1 - py, core), z)
    p_dev = (dev(px, py, 1 - core), z)
    up_dev = (gx, z + 1)
    dn_dev = (gx, z - 1)

    mirror = z // 2
    inner = z + (3 - 2 * z) * mirror

    def level(k):
        base = k + inner * (1 - 2 * k) * (1 - k // 2)
        return base + (3 - 2 * base) * mirror

    def block(plane, lev, c):
        return tok.at[plane, lev, pl.ds(c * rows, rows), :]

    def copy(src, dst, ssem, rsem, to):
        return pltpu.make_async_remote_copy(
            src_ref=src, dst_ref=dst, send_sem=ssem, recv_sem=rsem,
            device_id=to, device_id_type=MESH,
        )

    def piece_copy(j, k, h, ssem, to, src=None):
        lev = level(k)
        spot = tok.at[planes[j], lev, pl.ds(core * rows + h * half, half), :]
        start = spot if src is None else src.at[pl.ds(h * half, half), :]
        return copy(start, spot, ssem, recv.at[planes[j], lev, h], to)

    def partner_copy(j, k, src=None):
        lev = level(k)
        spot = block(planes[j], lev, core)
        return copy(spot if src is None else src, spot, s_p.at[j, k], precv.at[planes[j], lev], p_dev)

    def wait_piece(j, k, h):
        piece_copy(j, k, h, s_x.at[k, h], p_dev).wait_recv()

    def wait_partner(j, k):
        lev = level(k)
        spot = block(planes[j], lev, 1 - core)
        copy(spot, spot, s_p.at[j, k], precv.at[planes[j], lev], p_dev).wait_recv()

    def unit(j, k):
        wait_partner(j, k)
        lev = level(k)
        view = tok.at[planes[j], lev]
        named = view[:, pl.ds(width, LANES)].astype(jnp.float32)
        hit = jnp.max((named == expert.astype(jnp.float32)).astype(jnp.float32), axis=1, keepdims=True)
        cnt[...] += jnp.broadcast_to(jnp.sum(hit, axis=0, keepdims=True), cnt.shape)
        step = hid.shape[1] // 3

        def columns(n, carry):
            cols = pl.ds(pl.multiple_of(n * step, step), step)
            rows_in = view[:, pl.ds(0, width)]
            gate = jnp.dot(rows_in, wg[:, cols], preferred_element_type=jnp.float32)
            upward = jnp.dot(rows_in, wu[:, cols], preferred_element_type=jnp.float32)
            value = gate / (1.0 + jnp.exp(-gate)) * upward
            hid[:, cols] = jnp.where(hit > 0.5, value, 0.0).astype(jnp.bfloat16)
            return carry

        lax.fori_loop(0, 3, columns, 0)

        def bands(n, carry):
            cols = pl.ds(pl.multiple_of(n * step, step), step)
            acc[cols, :] += lax.dot_general(
                hid[:, cols], hid[...], (((0,), (0,)), ((), ())),
                preferred_element_type=jnp.float32,
            )
            return carry

        lax.fori_loop(0, 3, bands, 0)

    barrier = pltpu.get_barrier_semaphore()
    for to in (x_dev, y_dev, p_dev):
        pl.semaphore_signal(barrier, inc=1, device_id=to, device_id_type=MESH)

    @pl.when(z < 3)
    def _():
        pl.semaphore_signal(barrier, inc=1, device_id=up_dev, device_id_type=MESH)

    @pl.when(z > 0)
    def _():
        pl.semaphore_signal(barrier, inc=1, device_id=dn_dev, device_id_type=MESH)

    local = pltpu.make_async_copy(x_ref, block(here, z, core), l_sem.at[0])
    load_g = pltpu.make_async_copy(wg_hbm, wg, l_sem.at[1])
    load_u = pltpu.make_async_copy(wu_hbm, wu, l_sem.at[2])
    local.start()
    load_g.start()
    load_u.start()
    pl.semaphore_wait(barrier, 4 + inner)

    middle = inner == 1
    centre_dev = (gx, z + 1 - 2 * mirror)
    outer_dev = (gx, z - 1 + 2 * mirror)

    def sends_up(k):
        return jnp.logical_and(level(k) <= z, z < 3)

    def sends_down(k):
        return jnp.logical_and(level(k) >= z, z > 0)

    def along_z(k, h, act, src=None):
        @pl.when(sends_up(k))
        def _():
            act(piece_copy(0, k, h, s_up.at[k, h], up_dev, src))

        @pl.when(sends_down(k))
        def _():
            act(piece_copy(0, k, h, s_dn.at[k, h], dn_dev, src))

    def start(c):
        c.start()

    def sent(c):
        c.wait_send()

    def across(k, act, src=None):
        for h in range(2):
            act(piece_copy(0, k, h, s_y.at[k, h], y_dev, src))
            act(piece_copy(0, k, 1 - h, s_x.at[k, 1 - h], x_dev, src))

    def diag_x(k):
        return piece_copy(2, k, 0, s_dx.at[k], x_dev)

    def diag_y(k):
        return piece_copy(1, k, 1, s_dy.at[k], y_dev)

    def diag_z(k, h, to):
        return piece_copy(3, k, h, s_dz.at[k, h], to)

    def take_column(k):
        for h in range(2):
            wait_piece(0, k, h)

    def relay_column(k):
        for h in range(2):
            wait_piece(0, k, h)
            along_z(k, h, start)

    def relay_diag(k, to):
        for h in range(2):
            wait_piece(3, k, h)
            diag_z(k, h, to).start()

    for h in range(2):
        along_z(0, h, start, x_ref)
    across(0, start, x_ref)
    partner_copy(0, 0, x_ref).start()
    acc[...] = jnp.zeros_like(acc)
    cnt[...] = jnp.zeros_like(cnt)
    local.wait()
    load_g.wait()
    load_u.wait()

    def turn(k, carry):
        unit(0, k)

        @pl.when(k < 2)
        def _():
            wait_piece(2, k, 0)
            diag_x(k).start()
            wait_piece(1, k, 1)
            diag_y(k).start()

        @pl.when(jnp.logical_and(k < 3, jnp.logical_not(middle)))
        def _():
            take_column(k + 1)

        @pl.when(jnp.logical_and(k == 0, middle))
        def _():
            for h in range(2):
                for n in (1, 2):
                    wait_piece(0, n, h)
                    along_z(n, h, start)

        @pl.when(k < 3)
        def _():
            across(k + 1, start)
            partner_copy(0, k + 1).start()

        @pl.when(k >= 2)
        def _():
            wait_piece(2, k, 0)
            wait_piece(1, k, 1)

        wait_piece(2, k, 1)
        wait_piece(1, k, 0)
        partner_copy(1, k).start()
        partner_copy(2, k).start()
        unit(1, k)

        @pl.when(jnp.logical_and(k < 2, middle))
        def _():
            relay_diag(k, centre_dev)

        @pl.when(jnp.logical_and(k == 1, middle))
        def _():
            relay_diag(2, outer_dev)

        @pl.when(jnp.logical_and(k == 2, middle))
        def _():
            relay_diag(3, outer_dev)

        @pl.when(middle)
        def _():
            partner_copy(3, k).start()

        unit(2, k)

        @pl.when(jnp.logical_not(middle))
        def _():
            wait_piece(3, k, 0)
            wait_piece(3, k, 1)
            partner_copy(3, k).start()

        unit(3, k)

        @pl.when(jnp.logical_and(k == 0, middle))
        def _():
            relay_column(3)

        return carry

    lax.fori_loop(0, 4, turn, 0)
    out_ref[...] = acc[...] / cnt[0:1, 0:1]

    def drain(k, carry):
        for h in range(2):
            along_z(k, h, sent)
        across(k, sent)

        @pl.when(k < 2)
        def _():
            diag_x(k).wait_send()
            diag_y(k).wait_send()

        @pl.when(middle)
        def _():
            for h in range(2):
                diag_z(k, h, outer_dev).wait_send()

        for j in range(4):
            partner_copy(j, k).wait_send()
        return carry

    lax.fori_loop(0, 4, drain, 0)


def fused_local(tokens, expert_ids, w_gate, w_up, down_error):
    rows, width = tokens.shape
    hidden = w_gate.shape[2]
    named = jnp.pad(
        expert_ids.astype(jnp.bfloat16),
        ((0, 0), (0, LANES - expert_ids.shape[1])),
        constant_values=-1.0,
    )
    packed = jnp.concatenate([tokens, named], axis=1)
    vmem = pl.BlockSpec(memory_space=pltpu.VMEM)
    hbm = pl.BlockSpec(memory_space=pltpu.HBM)
    dma = pltpu.SemaphoreType.DMA
    mean_gram = pl.pallas_call(
        fused_kernel,
        out_shape=jax.ShapeDtypeStruct((hidden, hidden), jnp.float32),
        in_specs=[vmem, hbm, hbm],
        out_specs=vmem,
        scratch_shapes=[
            pltpu.VMEM((4, 4, 2 * rows, width + LANES), jnp.bfloat16),
            pltpu.VMEM((width, hidden), jnp.bfloat16),
            pltpu.VMEM((width, hidden), jnp.bfloat16),
            pltpu.VMEM((2 * rows, hidden), jnp.bfloat16),
            pltpu.VMEM((hidden, hidden), jnp.float32),
            pltpu.VMEM((8, LANES), jnp.float32),
            dma((4, 4, 2)), dma((4, 4)),
            dma((4, 2)), dma((4, 2)), dma((4,)), dma((4,)), dma((4, 2)),
            dma((4, 4)), dma((4, 2)), dma((4, 2)),
            dma((3,)),
        ],
        compiler_params=pltpu.CompilerParams(
            collective_id=0, has_side_effects=True, vmem_limit_bytes=56 * 1024 * 1024
        ),
    )(packed, w_gate[0], w_up[0])
    return jnp.dot(mean_gram, down_error[0], preferred_element_type=jnp.float32)[None]


def hidden_rows(received, w_gate, w_up):
    sources, slots, width = received.shape
    flat_rows = received.reshape(sources * slots, width)
    gate = jnp.dot(flat_rows, w_gate[0], preferred_element_type=jnp.float32)
    upward = jnp.dot(flat_rows, w_up[0], preferred_element_type=jnp.float32)
    hidden = (jax.nn.silu(gate) * upward).astype(jnp.bfloat16)
    return hidden.reshape(sources, slots, hidden.shape[1])


def cross_gram(first, second):
    return lax.dot_general(
        first, second, (((0,), (0,)), ((), ())), preferred_element_type=jnp.float32
    )


def gram_of(hidden):
    middle = hidden.shape[1] // 2
    left_part = hidden[:, :middle]
    right_part = hidden[:, middle:]
    upper_left = cross_gram(left_part, left_part)
    upper_right = cross_gram(left_part, right_part)
    lower_right = cross_gram(right_part, right_part)
    top_band = jnp.concatenate([upper_left, upper_right], axis=1)
    bottom_band = jnp.concatenate([upper_right.T, lower_right], axis=1)
    return jnp.concatenate([top_band, bottom_band], axis=0)


def local(tokens, expert_ids, w_gate, w_up, down_error):
    across = lax.axis_size("gx")
    within = lax.axis_size("gy")
    experts = across * within
    tok_count, top_count = expert_ids.shape
    width = tokens.shape[1]
    assigned = tok_count * top_count
    capacity = 3 * assigned // experts
    flat_ids = expert_ids.reshape(assigned)
    onehot = (flat_ids[:, None] == jnp.arange(experts, dtype=jnp.int32)[None, :]).astype(
        jnp.bfloat16
    )
    positions = jnp.arange(assigned, dtype=jnp.int32)
    lower = (positions[:, None] >= positions[None, :]).astype(jnp.bfloat16)
    running = jnp.dot(lower, onehot, preferred_element_type=jnp.float32)
    slot_of = (jnp.sum(running * onehot, axis=1) - 1.0).astype(jnp.int32)
    target = flat_ids * capacity + slot_of
    picked = tokens[positions // top_count]
    outgoing = jnp.zeros((experts * capacity, width), jnp.bfloat16).at[target].set(picked)
    tallies = jnp.sum(onehot.astype(jnp.float32), axis=0)
    loads = lax.psum_scatter(tallies, ("gx", "gy"), scatter_dimension=0, tiled=True)
    hidden = hidden_rows(
        lax.all_to_all(
            outgoing.reshape(experts, capacity, width),
            ("gx", "gy"),
            split_axis=0,
            concat_axis=0,
            tiled=True,
        ),
        w_gate,
        w_up,
    )
    hidden = hidden.reshape(experts * capacity, hidden.shape[2])
    gram = gram_of(hidden)
    mean_gram = gram / loads[0]
    product = jnp.dot(
        mean_gram,
        down_error[0],
        preferred_element_type=jnp.float32,
        precision=lax.Precision.HIGHEST,
    )
    return product[None]


def solution(mesh):
    small = mesh.shape["gx"] == 8 and mesh.shape["gy"] == 4
    return jax.shard_map(
        fused_local if small else local,
        mesh=mesh,
        in_specs=(
            P(("gx", "gy"), None),
            P(("gx", "gy"), None),
            P(("gx", "gy"), None, None),
            P(("gx", "gy"), None, None),
            P(("gx", "gy"), None, None),
        ),
        out_specs=P(("gx", "gy"), None, None),
        check_vma=False,
    )
```

```python
import jax
import jax.numpy as jnp
from jax import lax
from jax.experimental import pallas as pl
from jax.experimental.pallas import tpu as pltpu
from jax.sharding import PartitionSpec as P

MESH = pl.DeviceIdType.MESH
LANES = 128


def fused_kernel(
    x_ref, wg_hbm, wu_hbm, out_ref,
    tok, wg, wu, hid, acc, cnt,
    recv, precv, s_x, s_y, s_dx, s_dy, s_dz, s_p, s_up, s_dn, l_sem,
):
    gx = lax.axis_index("gx")
    z = lax.axis_index("gy")
    rows = x_ref.shape[0]
    half = rows // 2
    width = wg.shape[0]
    core = gx % 2
    px = (gx // 2) % 2
    py = gx // 4
    expert = gx * 4 + z

    def plane_of(a, b):
        return b * 2 + a

    here = plane_of(px, py)
    planes = (here, plane_of(1 - px, py), plane_of(px, 1 - py), plane_of(1 - px, 1 - py))

    def dev(a, b, c):
        return b * 4 + a * 2 + c

    x_dev = (dev(1 - px, py, core), z)
    y_dev = (dev(px, 1 - py, core), z)
    p_dev = (dev(px, py, 1 - core), z)
    up_dev = (gx, z + 1)
    dn_dev = (gx, z - 1)

    mirror = z // 2
    inner = z + (3 - 2 * z) * mirror

    def level(k):
        base = k + inner * (1 - 2 * k) * (1 - k // 2)
        return base + (3 - 2 * base) * mirror

    def block(plane, lev, c):
        return tok.at[plane, lev, pl.ds(c * rows, rows), :]

    def copy(src, dst, ssem, rsem, to):
        return pltpu.make_async_remote_copy(
            src_ref=src, dst_ref=dst, send_sem=ssem, recv_sem=rsem,
            device_id=to, device_id_type=MESH,
        )

    def piece_copy(j, k, h, ssem, to, src=None):
        lev = level(k)
        spot = tok.at[planes[j], lev, pl.ds(core * rows + h * half, half), :]
        start = spot if src is None else src.at[pl.ds(h * half, half), :]
        return copy(start, spot, ssem, recv.at[planes[j], lev, h], to)

    def partner_copy(j, k, src=None):
        lev = level(k)
        spot = block(planes[j], lev, core)
        return copy(spot if src is None else src, spot, s_p.at[j, k], precv.at[planes[j], lev], p_dev)

    def wait_piece(j, k, h):
        piece_copy(j, k, h, s_x.at[k, h], p_dev).wait_recv()

    def wait_partner(j, k):
        lev = level(k)
        spot = block(planes[j], lev, 1 - core)
        copy(spot, spot, s_p.at[j, k], precv.at[planes[j], lev], p_dev).wait_recv()

    def unit(j, k):
        wait_partner(j, k)
        lev = level(k)
        view = tok.at[planes[j], lev]
        named = view[:, pl.ds(width, LANES)].astype(jnp.float32)
        hit = jnp.max((named == expert.astype(jnp.float32)).astype(jnp.float32), axis=1, keepdims=True)
        cnt[...] += jnp.broadcast_to(jnp.sum(hit, axis=0, keepdims=True), cnt.shape)
        rows_in = view[:, pl.ds(0, width)]
        for n in range(bands):
            cols = pl.ds(n * step, step)
            gate = jnp.dot(rows_in, wg[:, cols], preferred_element_type=jnp.float32)
            upward = jnp.dot(rows_in, wu[:, cols], preferred_element_type=jnp.float32)
            value = gate / (1.0 + jnp.exp(-gate)) * upward
            hid[pl.ds((j % 2) * 2 * rows, 2 * rows), cols] = jnp.where(hit > 0.5, value, 0.0).astype(jnp.bfloat16)

    bands = 3
    step = hid.shape[1] // bands

    def gram():
        for n in range(bands):
            rest = pl.ds(n * step, hid.shape[1] - n * step)
            acc[pl.ds(n * step, step), rest] += lax.dot_general(
                hid[:, pl.ds(n * step, step)], hid[:, rest], (((0,), (0,)), ((), ())),
                preferred_element_type=jnp.float32,
            )

    barrier = pltpu.get_barrier_semaphore()
    for to in (x_dev, y_dev, p_dev):
        pl.semaphore_signal(barrier, inc=1, device_id=to, device_id_type=MESH)

    @pl.when(z < 3)
    def _():
        pl.semaphore_signal(barrier, inc=1, device_id=up_dev, device_id_type=MESH)

    @pl.when(z > 0)
    def _():
        pl.semaphore_signal(barrier, inc=1, device_id=dn_dev, device_id_type=MESH)

    local = pltpu.make_async_copy(x_ref, block(here, z, core), l_sem.at[0])
    load_g = pltpu.make_async_copy(wg_hbm, wg, l_sem.at[1])
    load_u = pltpu.make_async_copy(wu_hbm, wu, l_sem.at[2])
    local.start()
    load_g.start()
    load_u.start()
    pl.semaphore_wait(barrier, 4 + inner)

    middle = inner == 1
    centre_dev = (gx, z + 1 - 2 * mirror)
    outer_dev = (gx, z - 1 + 2 * mirror)

    def sends_up(k):
        return jnp.logical_and(level(k) <= z, z < 3)

    def sends_down(k):
        return jnp.logical_and(level(k) >= z, z > 0)

    def along_z(k, h, act, src=None):
        @pl.when(sends_up(k))
        def _():
            act(piece_copy(0, k, h, s_up.at[k, h], up_dev, src))

        @pl.when(sends_down(k))
        def _():
            act(piece_copy(0, k, h, s_dn.at[k, h], dn_dev, src))

    def start(c):
        c.start()

    def sent(c):
        c.wait_send()

    def across(k, act, src=None):
        for h in range(2):
            act(piece_copy(0, k, h, s_y.at[k, h], y_dev, src))
            act(piece_copy(0, k, 1 - h, s_x.at[k, 1 - h], x_dev, src))

    def diag_x(k):
        return piece_copy(2, k, 0, s_dx.at[k], x_dev)

    def diag_y(k):
        return piece_copy(1, k, 1, s_dy.at[k], y_dev)

    def diag_z(k, h, to):
        return piece_copy(3, k, h, s_dz.at[k, h], to)

    def take_column(k):
        for h in range(2):
            wait_piece(0, k, h)

    def relay_column(k):
        for h in range(2):
            wait_piece(0, k, h)
            along_z(k, h, start)

    def relay_diag(k, to):
        for h in range(2):
            wait_piece(3, k, h)
            diag_z(k, h, to).start()

    for h in range(2):
        along_z(0, h, start, x_ref)
    across(0, start, x_ref)
    partner_copy(0, 0, x_ref).start()
    acc[...] = jnp.zeros_like(acc)
    cnt[...] = jnp.zeros_like(cnt)
    local.wait()
    load_g.wait()
    load_u.wait()

    def turn(k, carry):
        unit(0, k)

        @pl.when(k < 2)
        def _():
            wait_piece(2, k, 0)
            diag_x(k).start()
            wait_piece(1, k, 1)
            diag_y(k).start()

        @pl.when(jnp.logical_and(k < 3, jnp.logical_not(middle)))
        def _():
            take_column(k + 1)

        @pl.when(jnp.logical_and(k == 0, middle))
        def _():
            for h in range(2):
                for n in (1, 2):
                    wait_piece(0, n, h)
                    along_z(n, h, start)

        @pl.when(k < 3)
        def _():
            across(k + 1, start)
            partner_copy(0, k + 1).start()

        @pl.when(k >= 2)
        def _():
            wait_piece(2, k, 0)
            wait_piece(1, k, 1)

        wait_piece(2, k, 1)
        wait_piece(1, k, 0)
        partner_copy(1, k).start()
        partner_copy(2, k).start()
        unit(1, k)
        gram()

        @pl.when(jnp.logical_and(k < 2, middle))
        def _():
            relay_diag(k, centre_dev)

        @pl.when(jnp.logical_and(k == 1, middle))
        def _():
            relay_diag(2, outer_dev)

        @pl.when(jnp.logical_and(k == 2, middle))
        def _():
            relay_diag(3, outer_dev)

        @pl.when(middle)
        def _():
            partner_copy(3, k).start()

        unit(2, k)

        @pl.when(jnp.logical_not(middle))
        def _():
            wait_piece(3, k, 0)
            wait_piece(3, k, 1)
            partner_copy(3, k).start()

        unit(3, k)
        gram()

        @pl.when(jnp.logical_and(k == 0, middle))
        def _():
            relay_column(3)

        return carry

    lax.fori_loop(0, 4, turn, 0)
    count = cnt[0:1, 0:1]
    for n in range(bands):
        for m in range(n, bands):
            part = acc[pl.ds(n * step, step), pl.ds(m * step, step)] / count
            out_ref[pl.ds(n * step, step), pl.ds(m * step, step)] = part
            if m > n:
                out_ref[pl.ds(m * step, step), pl.ds(n * step, step)] = part.T

    def drain(k, carry):
        for h in range(2):
            along_z(k, h, sent)
        across(k, sent)

        @pl.when(k < 2)
        def _():
            diag_x(k).wait_send()
            diag_y(k).wait_send()

        @pl.when(middle)
        def _():
            for h in range(2):
                diag_z(k, h, outer_dev).wait_send()

        for j in range(4):
            partner_copy(j, k).wait_send()
        return carry

    lax.fori_loop(0, 4, drain, 0)


def fused_local(tokens, expert_ids, w_gate, w_up, down_error):
    rows, width = tokens.shape
    hidden = w_gate.shape[2]
    named = jnp.pad(
        expert_ids.astype(jnp.bfloat16),
        ((0, 0), (0, LANES - expert_ids.shape[1])),
        constant_values=-1.0,
    )
    packed = jnp.concatenate([tokens, named], axis=1)
    vmem = pl.BlockSpec(memory_space=pltpu.VMEM)
    hbm = pl.BlockSpec(memory_space=pltpu.HBM)
    dma = pltpu.SemaphoreType.DMA
    mean_gram = pl.pallas_call(
        fused_kernel,
        out_shape=jax.ShapeDtypeStruct((hidden, hidden), jnp.float32),
        in_specs=[vmem, hbm, hbm],
        out_specs=vmem,
        scratch_shapes=[
            pltpu.VMEM((4, 4, 2 * rows, width + LANES), jnp.bfloat16),
            pltpu.VMEM((width, hidden), jnp.bfloat16),
            pltpu.VMEM((width, hidden), jnp.bfloat16),
            pltpu.VMEM((4 * rows, hidden), jnp.bfloat16),
            pltpu.VMEM((hidden, hidden), jnp.float32),
            pltpu.VMEM((8, LANES), jnp.float32),
            dma((4, 4, 2)), dma((4, 4)),
            dma((4, 2)), dma((4, 2)), dma((4,)), dma((4,)), dma((4, 2)),
            dma((4, 4)), dma((4, 2)), dma((4, 2)),
            dma((3,)),
        ],
        compiler_params=pltpu.CompilerParams(
            collective_id=0, has_side_effects=True, vmem_limit_bytes=56 * 1024 * 1024
        ),
    )(packed, w_gate[0], w_up[0])
    return jnp.dot(mean_gram, down_error[0], preferred_element_type=jnp.float32)[None]


def hidden_rows(received, w_gate, w_up):
    sources, slots, width = received.shape
    flat_rows = received.reshape(sources * slots, width)
    gate = jnp.dot(flat_rows, w_gate[0], preferred_element_type=jnp.float32)
    upward = jnp.dot(flat_rows, w_up[0], preferred_element_type=jnp.float32)
    hidden = (jax.nn.silu(gate) * upward).astype(jnp.bfloat16)
    return hidden.reshape(sources, slots, hidden.shape[1])


def cross_gram(first, second):
    return lax.dot_general(
        first, second, (((0,), (0,)), ((), ())), preferred_element_type=jnp.float32
    )


def gram_of(hidden):
    middle = hidden.shape[1] // 2
    left_part = hidden[:, :middle]
    right_part = hidden[:, middle:]
    upper_left = cross_gram(left_part, left_part)
    upper_right = cross_gram(left_part, right_part)
    lower_right = cross_gram(right_part, right_part)
    top_band = jnp.concatenate([upper_left, upper_right], axis=1)
    bottom_band = jnp.concatenate([upper_right.T, lower_right], axis=1)
    return jnp.concatenate([top_band, bottom_band], axis=0)


def local(tokens, expert_ids, w_gate, w_up, down_error):
    across = lax.axis_size("gx")
    within = lax.axis_size("gy")
    experts = across * within
    tok_count, top_count = expert_ids.shape
    width = tokens.shape[1]
    assigned = tok_count * top_count
    capacity = 3 * assigned // experts
    flat_ids = expert_ids.reshape(assigned)
    onehot = (flat_ids[:, None] == jnp.arange(experts, dtype=jnp.int32)[None, :]).astype(
        jnp.bfloat16
    )
    positions = jnp.arange(assigned, dtype=jnp.int32)
    lower = (positions[:, None] >= positions[None, :]).astype(jnp.bfloat16)
    running = jnp.dot(lower, onehot, preferred_element_type=jnp.float32)
    slot_of = (jnp.sum(running * onehot, axis=1) - 1.0).astype(jnp.int32)
    target = flat_ids * capacity + slot_of
    picked = tokens[positions // top_count]
    outgoing = jnp.zeros((experts * capacity, width), jnp.bfloat16).at[target].set(picked)
    tallies = jnp.sum(onehot.astype(jnp.float32), axis=0)
    loads = lax.psum_scatter(tallies, ("gx", "gy"), scatter_dimension=0, tiled=True)
    hidden = hidden_rows(
        lax.all_to_all(
            outgoing.reshape(experts, capacity, width),
            ("gx", "gy"),
            split_axis=0,
            concat_axis=0,
            tiled=True,
        ),
        w_gate,
        w_up,
    )
    hidden = hidden.reshape(experts * capacity, hidden.shape[2])
    gram = gram_of(hidden)
    mean_gram = gram / loads[0]
    product = jnp.dot(
        mean_gram,
        down_error[0],
        preferred_element_type=jnp.float32,
        precision=lax.Precision.HIGHEST,
    )
    return product[None]


def solution(mesh):
    small = mesh.shape["gx"] == 8 and mesh.shape["gy"] == 4
    return jax.shard_map(
        fused_local if small else local,
        mesh=mesh,
        in_specs=(
            P(("gx", "gy"), None),
            P(("gx", "gy"), None),
            P(("gx", "gy"), None, None),
            P(("gx", "gy"), None, None),
            P(("gx", "gy"), None, None),
        ),
        out_specs=P(("gx", "gy"), None, None),
        check_vma=False,
    )
```
